256 devices in a mesh: row: 16 (over z_lo, x), col: 16 (over z_hi, y, core).
Axes of the slice: x: 4, y: 4, z: 8 (z_hi: 2, z_lo: 4; z = z_hi * 4 + z_lo), core: 2. Of those that a mesh axis runs over, the one named last changes fastest.
Arguments:
- amplitudes: bfloat16 [65536, 768], P(('row', 'col')), may hold values from -6 to 6
- integrals: bfloat16 [65536, 768], P(('row', 'col')), may hold values from -0.21875 to 0.21875
- block_mask: int32 [512, 512], P('row'), may hold values from 0 to 1, as said below
- occ_energy: float32 [64], replicated, may hold values from -1.5 to -0.5
- vir_energy: float32 [1024], replicated, may hold values from 0.1 to 1.5
Outputs:
- update: bfloat16 [16, 16, 192, 128, 128], P('row', 'col')
The draws below stay inside these ranges and needn't reach their ends.
Inputs may be any that keep to these rules, and one draw needn't show every extreme that they name: block_mask is symmetric; among the 2 x 2 blocks (a, b) with the same a // 2 and b // 2 at most one is present, and for every a // 2 one block with b // 2 = a // 2 and b = a is present; for every cell (r, c) at most 192 of its blocks are present, with exactly 192 in some cell.
All inputs are finite; a program needn't handle non-finite values.
Results may differ from the reference program's by a relative error of at most 0.0049.
Values may be sent and summed in bfloat16 or wider, within the bound.
A program may use at most 64 MiB of HBM per device.

```python
import jax
import jax.numpy as jnp
from jax import lax

BLOCK = 128
SHARD_BLOCKS = 2
KC = 768
NV = 1024
TILES = 192
ROW_GROUPS = 16
COL_GROUPS = 16
MB = 512
CAP = 192
N = 65536
NOCC = 64
N_COL = 16


def draw_block_mask(key, part):
    coarse = MB // SHARD_BLOCKS
    split = SHARD_BLOCKS
    limit = min(TILES, coarse)
    partners = limit - 1
    key_order = jax.random.fold_in(key, 11)
    key_level = jax.random.fold_in(key, 23)
    key_fine = jax.random.fold_in(key, 37)
    order = jax.random.permutation(key_order, coarse).astype(jnp.int32)
    places = jnp.arange(coarse, dtype=jnp.int32)
    level = jax.random.randint(key_level, (coarse,), 1, partners + 1).astype(jnp.int32)
    level = jnp.where(places <= partners, partners, level)
    offset = jnp.bitwise_xor(places[:, None], places[None, :])
    lowest = jnp.minimum(level[:, None], level[None, :])
    linked = (offset == 0) | (offset >= 1) & (offset <= lowest)
    inverse = jnp.argsort(order).astype(jnp.int32)
    graph = linked[inverse][:, inverse]
    first = places[:, None]
    second = places[None, :]
    source = first // N_COL * N_COL + second % N_COL
    target = second // N_COL * N_COL + first % N_COL
    coarse_mask = graph[source, target].astype(jnp.int32)
    choose = jax.random.randint(key_fine, (coarse, coarse), 0, split * split).astype(jnp.int32)
    upper = first <= second
    sym = jnp.where(upper, choose, choose.T)
    lead = sym // split
    trail = sym % split
    pick_row = jnp.where(first < second, lead, jnp.where(first > second, trail, lead))
    pick_col = jnp.where(first < second, trail, jnp.where(first > second, lead, lead))
    fine = jnp.arange(MB, dtype=jnp.int32)
    big_row = fine[:, None] // split
    big_col = fine[None, :] // split
    hit = (fine[:, None] % split == pick_row[big_row, big_col]) & (fine[None, :] % split == pick_col[big_row, big_col])
    return (coarse_mask[big_row, big_col] * hit.astype(jnp.int32)).astype(jnp.int32)


def shard_levels(rng, dims, cuts, least, largest):
    level, own = 1.0, jax.random.fold_in(rng, 6)
    for axis_at, parts in cuts:
        heights = jnp.exp(jax.random.uniform(jax.random.fold_in(own, axis_at), (parts,), jnp.float32, least / len(cuts), largest / len(cuts)))
        level = level * jnp.repeat(heights, dims[axis_at] // parts).reshape([-1 if axis == axis_at else 1 for axis in range(len(dims))])
    return level


def centred(rng, shape, deviation, bound, pieces=(), kind=jnp.bfloat16):
    drawn = deviation * jax.random.normal(rng, shape, jnp.float32)
    if pieces:
        drawn = drawn * shard_levels(rng, shape, pieces, -0.22, 0.18)
    return jnp.clip(drawn, -bound, bound).astype(kind)


def setup_inputs(seed: int = 0) -> dict:
    key_of = jax.random.split(jax.random.key(seed), 6)
    amplitudes = centred(key_of[0], (N, KC), 1.0, 6.0, ((0, 256),))
    integrals = centred(key_of[1], (N, KC), KC ** -0.5, 0.21875, ((0, 256),))
    block_mask = draw_block_mask(jax.random.fold_in(key_of[5], 71), 0)
    occ_energy = jnp.clip(jax.random.uniform(key_of[3], (NOCC,), jnp.float32, -1.5, -0.5), -1.5, -0.5)
    vir_energy = jnp.clip(jax.random.uniform(key_of[4], (NV,), jnp.float32, 0.1, 1.5), 0.1, 1.5)
    return {"amplitudes": amplitudes, "integrals": integrals, "block_mask": block_mask, "occ_energy": occ_energy, "vir_energy": vir_energy}


def slot_layout(block_mask, row_at, col_at, nrow, ncol, split, limit):
    rows_mask = lax.dynamic_slice_in_dim(block_mask, (row_at * ncol * split).astype(jnp.int32), ncol * split, 0)
    tile_mask = lax.dynamic_index_in_dim(rows_mask.reshape(ncol * split, nrow, ncol, split), col_at, 2, keepdims=False)
    flat = tile_mask.reshape(-1)
    wide = nrow * split
    cells = ncol * split * wide
    places = jnp.arange(cells, dtype=jnp.int32)
    keys = jnp.where(flat > 0, places, places + cells)
    picked = jnp.argsort(keys, stable=True)[:limit].astype(jnp.int32)
    present = flat[picked] > 0
    return picked // wide, picked % wide, present


def reference(amplitudes, integrals, block_mask, occ_energy, vir_energy):
    nrow = ROW_GROUPS
    ncol = COL_GROUPS
    split = SHARD_BLOCKS
    cells = nrow * ncol
    amp_blocks = amplitudes.reshape(MB, BLOCK, KC)
    int_blocks = integrals.reshape(MB, BLOCK, KC)
    gaps = (vir_energy[None, :] - occ_energy[:, None]).reshape(MB, BLOCK)

    def one_cell(cell):
        row_at = cell // ncol
        col_at = cell % ncol
        upick, vpick, present = slot_layout(block_mask, row_at, col_at, nrow, ncol, split, CAP)
        row_block = row_at * ncol * split + upick
        col_block = ((vpick // split) * ncol + col_at) * split + vpick % split
        direct = jnp.einsum("sik,sjk->sij", amp_blocks[row_block].astype(jnp.float32), int_blocks[col_block].astype(jnp.float32)).astype(jnp.bfloat16)
        mirror = jnp.einsum("sik,sjk->sij", amp_blocks[col_block].astype(jnp.float32), int_blocks[row_block].astype(jnp.float32)).astype(jnp.bfloat16)
        mirror = jnp.swapaxes(mirror, 1, 2)
        denom = gaps[row_block][:, :, None] + gaps[col_block][:, None, :]
        total = (direct.astype(jnp.float32) + mirror.astype(jnp.float32)) / denom
        return jnp.where(present[:, None, None], total, jnp.float32(0.0)).astype(jnp.bfloat16)

    result = lax.map(one_cell, jnp.arange(cells, dtype=jnp.int32))
    return result.reshape(nrow, ncol, CAP, BLOCK, BLOCK)
```

```python
import functools

import jax
import jax.numpy as jnp
from jax import lax
from jax.experimental import pallas as pl
from jax.experimental.pallas import tpu as pltpu
from jax.sharding import PartitionSpec as P

BLOCK = 128
UNIT = 256
DEPTH = 768
TILES = 192
GRID = 16
CELLS = GRID * GRID
MESH = pl.DeviceIdType.MESH

OWN = 6
CROSS = 7
UNITS = 19


def table(at, values):
    out = jnp.int32(values[0])
    for i in range(1, len(values)):
        out = jnp.where(at == i, jnp.int32(values[i]), out)
    return out


def names():
    keys = []
    for flow in (0, 1):
        for dist in (1, 2, 3):
            for piece in (0, 1):
                keys.append(("z", flow, dist, piece))
        keys.append(("z", flow, 4, flow))
    for k in range(4):
        for flow in (0, 1):
            for piece in (0, 1):
                keys.append(("x", k, flow, piece))
            keys.append(("xf", k, flow))
    for h in (0, 1):
        for flow in (0, 1):
            for piece in (0, 1):
                keys.append(("y", h, flow, piece))
            keys.append(("yf", h, flow))
        for dy in range(4):
            for piece in (0, 1):
                keys.append(("c", h, dy, piece))
    return {key: i for i, key in enumerate(keys)}


KEYS = names()


def exchange(pick, amp, ints, side_of, grow, gcol, dense, store, near, far, gaps, stage, local_sem, send_sem, recv_sem, out_sem):
    row, col = lax.axis_index("row"), lax.axis_index("col")
    zl, x = row // 4, row % 4
    zh, y, core = col // 8, (col // 2) % 4, col % 2
    z = zh * 4 + zl

    def at_x(step):
        return (zl * 4 + (x + step) % 4, col)

    def at_y(step):
        return (row, zh * 8 + ((y + step) % 4) * 2 + core)

    def at_z(step):
        there = (z + step) % 8
        return ((there % 4) * 4 + x, (there // 4) * 8 + y * 2 + core)

    partner = (row, zh * 8 + y * 2 + (1 - core))
    step_of = (1, 3)
    ring_of = (1, 7)

    own_copies = []
    for piece, src in enumerate((amp, ints)):
        own_copies.append(pltpu.make_async_copy(src, near.at[0, piece], local_sem.at[piece]))
        own_copies.append(pltpu.make_async_copy(src, store.at[OWN, piece], local_sem.at[2 + piece]))
    for copy in own_copies:
        copy.start()

    barrier = pltpu.get_barrier_semaphore()
    for there in (at_x(1), at_x(3), at_y(1), at_y(3), at_z(1), at_z(7), partner):
        pl.semaphore_signal(barrier, inc=1, device_id=there, device_id_type=MESH)
    pl.semaphore_wait(barrier, 7)
    for copy in own_copies:
        copy.wait()

    slot_k = [OWN] + [table(zl, v) for v in ((3, 0, 3, 0), (4, 3, 0, 1), (5, 4, 1, 2))]
    line_k = [zl] + [table(zl, v) for v in ((1, 0, 3, 2), (2, 2, 1, 1), (3, 3, 0, 0))]

    started = []

    def descriptor(key):
        i = KEYS[key]
        kind = key[0]
        if kind == "z":
            _, flow, dist, piece = key
            src = near.at[0, piece] if dist == 1 else store.at[flow * 3 + dist - 2, piece]
            dst = far.at[0, piece] if dist == 4 else store.at[flow * 3 + dist - 1, piece]
            there = at_z(ring_of[flow])
        elif kind == "x":
            _, k, flow, piece = key
            src = store.at[slot_k[k], piece]
            dst = store.at[CROSS + (2 if flow == 0 else 0) * 4 + k, piece]
            there = at_x(step_of[flow])
        elif kind == "xf":
            _, k, flow = key
            src = store.at[CROSS + (2 if flow == 0 else 0) * 4 + k, flow]
            dst = store.at[CROSS + 1 * 4 + k, flow]
            there = at_x(step_of[flow])
        elif kind == "y":
            _, h, flow, piece = key
            half = (near, far)[h]
            src = half.at[0, piece]
            dst = half.at[(3 if flow == 0 else 1) * 2, piece]
            there = at_y(step_of[flow])
        elif kind == "yf":
            _, h, flow = key
            half = (near, far)[h]
            src = half.at[(3 if flow == 0 else 1) * 2, flow]
            dst = half.at[2 * 2, flow]
            there = at_y(step_of[flow])
        else:
            _, h, dy, piece = key
            half = (near, far)[h]
            src = half.at[dy * 2, piece]
            dst = half.at[dy * 2 + 1, piece]
            there = partner
        return pltpu.make_async_remote_copy(
            src_ref=src,
            dst_ref=dst,
            send_sem=send_sem.at[i],
            recv_sem=recv_sem.at[i],
            device_id=there,
            device_id_type=MESH,
        )

    def send(*key):
        copy = descriptor(key)
        copy.start()
        started.append(copy)

    def got(*key):
        descriptor(key).wait_recv()

    def send_unit(kind, at):
        for i in (0, 1):
            send(kind, at, 0, i)
            send(kind, at, 1, 1 - i)

    def chunk(n, half, unit, there):
        rows_ref = (near, far)[half]
        side = zh if half == 0 else 1 - zh

        def one(i, carry):
            place = ((y + i // 2) % 4) * 2 + (core + i % 2) % 2
            upper = side * 8 + place
            at = there * GRID + upper
            p = pick[at]
            dims = (((1,), (1,)), ((), ()))
            both = lax.dot_general(
                rows_ref[i, 0, p],
                store[unit, 1].reshape(UNIT, DEPTH),
                dims,
                preferred_element_type=jnp.float32,
            ) + lax.dot_general(
                rows_ref[i, 1, p],
                store[unit, 0].reshape(UNIT, DEPTH),
                dims,
                preferred_element_type=jnp.float32,
            )
            second = jnp.broadcast_to(side_of[at], (BLOCK, BLOCK)) > 0.5
            kept = jnp.where(second, both[:, BLOCK:], both[:, :BLOCK])
            below = gaps[pick[CELLS + at]] + gcol[pick[2 * CELLS + at]]
            stage[n, place] = (kept / below).astype(jnp.bfloat16)
            return carry

        lax.fori_loop(0, 8, one, 0)
        pltpu.make_async_copy(stage.at[n], dense.at[pl.ds(there * GRID + side * 8, 8)], out_sem.at[n]).start()
        outs.append((n, there, side))

    outs = []
    count = iter(range(32))

    def compute(half, k, dx):
        unit = slot_k[k] if dx == 0 else CROSS + (dx - 1) * 4 + k
        chunk(next(count), half, unit, line_k[k] * 4 + (x + dx) % 4)

    def half_ready(h):
        for dy in range(4):
            for piece in (0, 1):
                got("c", h, dy, piece)

    for i in (0, 1):
        send("z", 0, 1, i)
        send("z", 1, 1, 1 - i)
        send("x", 0, 0, i)
        send("x", 0, 1, 1 - i)
        send("y", 0, 0, i)
        send("y", 0, 1, 1 - i)
    send("c", 0, 0, 0)
    send("c", 0, 0, 1)
    for u in range(32):
        gaps[u] = jnp.broadcast_to(grow[:, u : u + 1], (BLOCK, BLOCK))
    stage[32] = jnp.zeros((8, BLOCK, BLOCK), jnp.bfloat16)
    zero = pltpu.make_async_copy(stage.at[32], dense.at[pl.ds(CELLS, 8)], local_sem.at[4])
    zero.start()
    for flow in (0, 1):
        got("z", flow, 1, flow)
        send("z", flow, 2, flow)
        got("x", 0, flow, flow)
        send("xf", 0, flow)
        got("y", 0, flow, flow)
        send("yf", 0, flow)
    for flow in (0, 1):
        got("z", flow, 1, 1 - flow)
        send("z", flow, 2, 1 - flow)
    send_unit("x", 1)
    for flow in (0, 1):
        got("y", 0, flow, 1 - flow)
    for dy in (1, 3):
        send("c", 0, dy, 0)
        send("c", 0, dy, 1)
    for flow in (0, 1):
        got("z", flow, 2, flow)
        send("z", flow, 3, flow)
    for flow in (0, 1):
        got("yf", 0, flow)
        send("c", 0, 2, flow)
    half_ready(0)
    compute(0, 0, 0)
    for flow in (0, 1):
        got("z", flow, 2, 1 - flow)
        send("z", flow, 3, 1 - flow)
    send_unit("x", 2)
    for flow in (0, 1):
        got("x", 1, flow, flow)
        send("xf", 1, flow)
    for flow in (0, 1):
        got("x", 0, flow, 1 - flow)
    compute(0, 0, 1)
    compute(0, 0, 3)
    for flow in (0, 1):
        got("z", flow, 3, flow)
        send("z", flow, 4, flow)
    for flow in (0, 1):
        got("xf", 0, flow)
    compute(0, 0, 2)
    compute(0, 1, 0)
    for flow in (0, 1):
        got("z", flow, 3, 1 - flow)
    send_unit("x", 3)
    for flow in (0, 1):
        got("x", 1, flow, 1 - flow)
    compute(0, 1, 1)
    compute(0, 1, 3)
    for flow in (0, 1):
        got("z", flow, 4, flow)
    send_unit("y", 1)
    send("c", 1, 0, 0)
    send("c", 1, 0, 1)
    for flow in (0, 1):
        got("x", 2, flow, flow)
        send("xf", 2, flow)
    for flow in (0, 1):
        got("xf", 1, flow)
    compute(0, 1, 2)
    compute(0, 2, 0)
    for flow in (0, 1):
        got("y", 1, flow, flow)
        send("yf", 1, flow)
    for flow in (0, 1):
        got("x", 2, flow, 1 - flow)
    compute(0, 2, 1)
    compute(0, 2, 3)
    for flow in (0, 1):
        got("y", 1, flow, 1 - flow)
    for dy in (1, 3):
        send("c", 1, dy, 0)
        send("c", 1, dy, 1)
    for flow in (0, 1):
        got("xf", 2, flow)
    compute(0, 2, 2)
    compute(0, 3, 0)
    for flow in (0, 1):
        got("x", 3, flow, flow)
        send("xf", 3, flow)
    for flow in (0, 1):
        got("yf", 1, flow)
        send("c", 1, 2, flow)
    half_ready(1)
    for k in range(4):
        compute(1, k, 0)
    for k in range(3):
        for dx in (1, 3, 2):
            compute(1, k, dx)
    for flow in (0, 1):
        got("x", 3, flow, 1 - flow)
    for dx in (1, 3):
        compute(0, 3, dx)
        compute(1, 3, dx)
    for flow in (0, 1):
        got("xf", 3, flow)
    compute(0, 3, 2)
    compute(1, 3, 2)

    for copy in started:
        copy.wait_send()
    zero.wait()
    for n, there, side in outs:
        pltpu.make_async_copy(stage.at[n], dense.at[pl.ds(there * GRID + side * 8, 8)], out_sem.at[n]).wait()


def products(pick, amplitudes, integrals, side_of, grow, gcol):
    anywhere = pl.BlockSpec(memory_space=pl.ANY)
    vmem = pl.BlockSpec(memory_space=pltpu.VMEM)
    pairs = len(KEYS)
    return pl.pallas_call(
        exchange,
        out_shape=jax.ShapeDtypeStruct((CELLS + 8, BLOCK, BLOCK), jnp.bfloat16),
        in_specs=[pl.BlockSpec(memory_space=pltpu.SMEM), anywhere, anywhere, vmem, vmem, vmem],
        out_specs=anywhere,
        scratch_shapes=[
            pltpu.VMEM((UNITS, 2, 2, BLOCK, DEPTH), jnp.bfloat16),
            pltpu.VMEM((8, 2, 2, BLOCK, DEPTH), jnp.bfloat16),
            pltpu.VMEM((8, 2, 2, BLOCK, DEPTH), jnp.bfloat16),
            pltpu.VMEM((32, BLOCK, BLOCK), jnp.float32),
            pltpu.VMEM((33, 8, BLOCK, BLOCK), jnp.bfloat16),
            pltpu.SemaphoreType.DMA((5,)),
            pltpu.SemaphoreType.DMA((pairs,)),
            pltpu.SemaphoreType.DMA((pairs,)),
            pltpu.SemaphoreType.DMA((32,)),
        ],
        compiler_params=pltpu.CompilerParams(
            collective_id=0, has_side_effects=True, vmem_limit_bytes=60 * 1024 * 1024
        ),
        name="exchange",
    )(pick, amplitudes, integrals, side_of, grow, gcol)


def ordered(places, dense, out, held, in_sem, out_sem):
    group = 16
    groups = TILES // group

    def read(g, j):
        return pltpu.make_async_copy(dense.at[places[g * group + j]], held.at[g * group + j], in_sem.at[g * group + j])

    def write(g):
        rows = pl.ds(g * group, group)
        return pltpu.make_async_copy(held.at[rows], out.at[0, 0, rows], out_sem.at[g])

    for g in range(groups):
        for j in range(group):
            read(g, j).start()
    for g in range(groups):
        for j in range(group):
            read(g, j).wait()
        write(g).start()
    for g in range(groups):
        write(g).wait()


def in_order(places, dense):
    anywhere = pl.BlockSpec(memory_space=pl.ANY)
    return pl.pallas_call(
        ordered,
        out_shape=jax.ShapeDtypeStruct((1, 1, TILES, BLOCK, BLOCK), jnp.bfloat16),
        in_specs=[pl.BlockSpec(memory_space=pltpu.SMEM), anywhere],
        out_specs=anywhere,
        scratch_shapes=[
            pltpu.VMEM((TILES, BLOCK, BLOCK), jnp.bfloat16),
            pltpu.SemaphoreType.DMA((TILES,)),
            pltpu.SemaphoreType.DMA((12,)),
        ],
        name="ordered",
    )(places, dense)


def shards(amplitudes, integrals, block_mask, occ_energy, vir_energy):
    row, col = lax.axis_index("row"), lax.axis_index("col")
    cell = lax.dynamic_index_in_dim(block_mask.reshape(32, GRID, GRID, 2), col, 2, keepdims=False)
    four = cell.reshape(GRID, 2, GRID, 2)
    low = jnp.max(four[:, 1], axis=2).T
    right = jnp.max(four[..., 1], axis=1).T
    line = jnp.arange(GRID, dtype=jnp.int32)
    pick = jnp.stack([low, line[None, :] * 2 + low, line[:, None] * 2 + right]).reshape(3 * CELLS)
    side_of = jnp.broadcast_to(right.astype(jnp.float32).reshape(CELLS, 1, 1), (CELLS, 1, BLOCK))

    flat = cell.reshape(32, 32).astype(jnp.float32)
    at = jnp.arange(32)
    inside = flat @ (at[:, None] <= at[None, :]).astype(jnp.float32)
    ahead = (at[None, :] < at[:, None]).astype(jnp.float32) @ inside[:, 31:]
    ranks = (inside + ahead).astype(jnp.int32).reshape(1024)
    slot = jnp.arange(TILES, dtype=jnp.int32)
    where = jnp.sum((ranks[None, :] <= slot[:, None]).astype(jnp.int32), axis=1)
    dense_at = (where % 32) // 2 * GRID + where // 64
    places = jnp.where(slot < ranks[1023], dense_at, CELLS)

    blocks = row * 32 + jnp.arange(32, dtype=jnp.int32)
    levels = vir_energy.reshape(8, BLOCK)
    grow = (levels[blocks % 8] - occ_energy[blocks // 8][:, None]).T
    blocks = (jnp.arange(32, dtype=jnp.int32) // 2 * GRID + col) * 2 + jnp.arange(32, dtype=jnp.int32) % 2
    gcol = (levels[blocks % 8] - occ_energy[blocks // 8][:, None]).reshape(32, 1, BLOCK)

    dense = products(
        pick, amplitudes.reshape(2, BLOCK, DEPTH), integrals.reshape(2, BLOCK, DEPTH), side_of, grow, gcol
    )
    return in_order(places, dense)


def solution(mesh):
    in_specs = (P(("row", "col"), None), P(("row", "col"), None), P("row", None), P(), P())
    out_specs = P("row", "col", None, None, None)
    return jax.shard_map(shards, mesh=mesh, in_specs=in_specs, out_specs=out_specs, check_vma=False)
```

```python
import functools

import jax
import jax.numpy as jnp
from jax import lax
from jax.experimental import pallas as pl
from jax.experimental.pallas import tpu as pltpu
from jax.sharding import PartitionSpec as P

BLOCK = 128
UNIT = 256
DEPTH = 768
TILES = 192
GRID = 16
CELLS = GRID * GRID
MESH = pl.DeviceIdType.MESH

OWN = 6
CROSS = 7
UNITS = 19
LIMIT = 46 * 1024 * 1024


def table(at, values):
    out = jnp.int32(values[0])
    for i in range(1, len(values)):
        out = jnp.where(at == i, jnp.int32(values[i]), out)
    return out


def names():
    keys = []
    for flow in (0, 1):
        for dist in (1, 2, 3):
            for piece in (0, 1):
                keys.append(("z", flow, dist, piece))
        keys.append(("z", flow, 4, flow))
    for k in range(4):
        for flow in (0, 1):
            for piece in (0, 1):
                keys.append(("x", k, flow, piece))
            keys.append(("xf", k, flow))
    for h in (0, 1):
        for flow in (0, 1):
            for piece in (0, 1):
                keys.append(("y", h, flow, piece))
            keys.append(("yf", h, flow))
        for dy in range(4):
            for piece in (0, 1):
                keys.append(("c", h, dy, piece))
    return {key: i for i, key in enumerate(keys)}


KEYS = names()


def exchange(
    low_s, amp, ints, side_of, occ, vir_all, dense,
    store, near, far, last, gaps, vir, occ_s,
    local_sem, send_sem, recv_sem,
):
    row, col = lax.axis_index("row"), lax.axis_index("col")
    zl, x = row // 4, row % 4
    zh, y, core = col // 8, (col // 2) % 4, col % 2
    z = zh * 4 + zl

    def at_x(step):
        return (zl * 4 + (x + step) % 4, col)

    def at_y(step):
        return (row, zh * 8 + ((y + step) % 4) * 2 + core)

    def at_z(step):
        there = (z + step) % 8
        return ((there % 4) * 4 + x, (there // 4) * 8 + y * 2 + core)

    partner = (row, zh * 8 + y * 2 + (1 - core))
    step_of = (1, 3)
    ring_of = (1, 7)

    own_copies = []
    for piece, src in enumerate((amp, ints)):
        own_copies.append(pltpu.make_async_copy(src, near.at[0, piece], local_sem.at[piece]))
        own_copies.append(pltpu.make_async_copy(src, store.at[OWN, piece], local_sem.at[2 + piece]))
    for copy in own_copies:
        copy.start()
    occ_copy = pltpu.make_async_copy(occ, occ_s, local_sem.at[5])
    occ_copy.start()
    vir_copy = pltpu.make_async_copy(vir_all, vir, local_sem.at[7])
    vir_copy.start()

    barrier = pltpu.get_barrier_semaphore()
    for there in (at_x(1), at_x(3), at_y(1), at_y(3), at_z(1), at_z(7), partner):
        pl.semaphore_signal(barrier, inc=1, device_id=there, device_id_type=MESH)
    pl.semaphore_wait(barrier, 7)
    for copy in (*own_copies, vir_copy):
        copy.wait()

    slot_k = [OWN] + [table(zl, v) for v in ((3, 0, 3, 0), (4, 3, 0, 1), (5, 4, 1, 2))]
    line_k = [zl] + [table(zl, v) for v in ((1, 0, 3, 2), (2, 2, 1, 1), (3, 3, 0, 0))]

    def rows_at(h, dy, dc, piece):
        if h == 0:
            return near.at[dy * 2 + dc, piece]
        return last.at[dc, piece] if dy == 2 else far.at[(0, 1, 0, 2)[dy] * 2 + dc, piece]

    started = []

    def descriptor(key):
        i = KEYS[key]
        kind = key[0]
        if kind == "z":
            _, flow, dist, piece = key
            src = rows_at(0, 0, 0, piece) if dist == 1 else store.at[flow * 3 + dist - 2, piece]
            dst = rows_at(1, 0, 0, piece) if dist == 4 else store.at[flow * 3 + dist - 1, piece]
            there = at_z(ring_of[flow])
        elif kind == "x":
            _, k, flow, piece = key
            src = store.at[slot_k[k], piece]
            dst = store.at[CROSS + (2 if flow == 0 else 0) * 4 + k, piece]
            there = at_x(step_of[flow])
        elif kind == "xf":
            _, k, flow = key
            src = store.at[CROSS + (2 if flow == 0 else 0) * 4 + k, flow]
            dst = store.at[CROSS + 1 * 4 + k, flow]
            there = at_x(step_of[flow])
        elif kind == "y":
            _, h, flow, piece = key
            src = rows_at(h, 0, 0, piece)
            dst = rows_at(h, 3 if flow == 0 else 1, 0, piece)
            there = at_y(step_of[flow])
        elif kind == "yf":
            _, h, flow = key
            src = rows_at(h, 3 if flow == 0 else 1, 0, flow)
            dst = rows_at(h, 2, 0, flow)
            there = at_y(step_of[flow])
        else:
            _, h, dy, piece = key
            src = rows_at(h, dy, 0, piece)
            dst = rows_at(h, dy, 1, piece)
            there = partner
        return pltpu.make_async_remote_copy(
            src_ref=src,
            dst_ref=dst,
            send_sem=send_sem.at[i],
            recv_sem=recv_sem.at[i],
            device_id=there,
            device_id_type=MESH,
        )

    def send(*key):
        copy = descriptor(key)
        copy.start()
        started.append(copy)

    def got(*key):
        descriptor(key).wait_recv()

    def send_unit(kind, at):
        for i in (0, 1):
            send(kind, at, 0, i)
            send(kind, at, 1, 1 - i)

    groups = (
        (near, 0, [(dy, dc) for dy in range(4) for dc in (0, 1)]),
        (far, 1, [(dy, dc) for dy in (0, 1, 3) for dc in (0, 1)]),
        (last, 1, [(2, dc) for dc in (0, 1)]),
    )
    first_line = vir[pl.ds((2 * col) % 8, 1), :]
    second_line = vir[pl.ds((2 * col + 1) % 8, 1), :]

    def chunk(group, k, dx):
        rows_ref, half, members = groups[group]
        unit = slot_k[k] if dx == 0 else CROSS + (dx - 1) * 4 + k
        there = line_k[k] * 4 + (x + dx) % 4
        side = zh if half == 0 else 1 - zh
        places = [((y + dy) % 4) * 2 + (core + dc) % 2 for dy, dc in members]
        ats = [there * GRID + side * 8 + p for p in places]
        lows = [low_s[at] for at in ats]
        dims = (((1,), (1,)), ((), ()))
        both = [
            lax.dot_general(
                jnp.concatenate([rows_ref[i, piece, low] for i, low in enumerate(lows)], axis=0),
                store[unit, 1 - piece].reshape(UNIT, DEPTH),
                dims,
                preferred_element_type=jnp.float32,
            )
            for piece in (0, 1)
        ]
        both = both[0] + both[1]
        level = occ_s[there * 4 + col // 4]
        for i, (place, at) in enumerate(zip(places, ats)):
            mine = both[i * BLOCK : (i + 1) * BLOCK]
            right = side_of[at]
            across = jnp.where(right > 0.5, second_line, first_line) - level
            kept = jnp.where(jnp.broadcast_to(right, (BLOCK, BLOCK)) > 0.5, mine[:, BLOCK:], mine[:, :BLOCK])
            below = gaps[(side * 8 + place) * 2 + lows[i]] + across
            dense[at] = (kept / below).astype(jnp.bfloat16)

    def compute(group, *todo):
        for first, step, count in todo:
            for at in range(first, first + step * count, step):
                chunk(group, at // 4, at % 4)

    def half_ready(h, dys):
        for dy in dys:
            for piece in (0, 1):
                got("c", h, dy, piece)

    for i in (0, 1):
        send("z", 0, 1, i)
        send("z", 1, 1, 1 - i)
        send("x", 0, 0, i)
        send("x", 0, 1, 1 - i)
        send("y", 0, 0, i)
        send("y", 0, 1, 1 - i)
    send("c", 0, 0, 0)
    send("c", 0, 0, 1)
    occ_copy.wait()
    for j in range(8):
        turned = jnp.broadcast_to(vir[j : j + 1, :], (BLOCK, BLOCK)).T
        for t in range(4):
            gaps[j + 8 * t] = turned - occ_s[row * 4 + t]
    dense[CELLS] = jnp.zeros((BLOCK, BLOCK), jnp.bfloat16)
    for flow in (0, 1):
        got("z", flow, 1, flow)
        send("z", flow, 2, flow)
        got("x", 0, flow, flow)
        send("xf", 0, flow)
        got("y", 0, flow, flow)
        send("yf", 0, flow)
    for flow in (0, 1):
        got("z", flow, 1, 1 - flow)
        send("z", flow, 2, 1 - flow)
    send_unit("x", 1)
    for flow in (0, 1):
        got("y", 0, flow, 1 - flow)
    for dy in (1, 3):
        send("c", 0, dy, 0)
        send("c", 0, dy, 1)
    for flow in (0, 1):
        got("z", flow, 2, flow)
        send("z", flow, 3, flow)
    for flow in (0, 1):
        got("yf", 0, flow)
        send("c", 0, 2, flow)
    half_ready(0, range(4))
    compute(0, (0, 1, 1))
    for flow in (0, 1):
        got("z", flow, 2, 1 - flow)
        send("z", flow, 3, 1 - flow)
    send_unit("x", 2)
    for flow in (0, 1):
        got("x", 1, flow, flow)
        send("xf", 1, flow)
    for flow in (0, 1):
        got("x", 0, flow, 1 - flow)
    compute(0, (1, 2, 2))
    for flow in (0, 1):
        got("z", flow, 3, flow)
        send("z", flow, 4, flow)
    for flow in (0, 1):
        got("xf", 0, flow)
    compute(0, (2, 2, 2))
    for flow in (0, 1):
        got("z", flow, 3, 1 - flow)
    send_unit("x", 3)
    for flow in (0, 1):
        got("x", 1, flow, 1 - flow)
    compute(0, (5, 2, 2))
    for flow in (0, 1):
        got("z", flow, 4, flow)
    send_unit("y", 1)
    send("c", 1, 0, 0)
    send("c", 1, 0, 1)
    for flow in (0, 1):
        got("x", 2, flow, flow)
        send("xf", 2, flow)
    for flow in (0, 1):
        got("xf", 1, flow)
    compute(0, (6, 2, 2))
    for flow in (0, 1):
        got("y", 1, flow, flow)
        send("yf", 1, flow)
    for flow in (0, 1):
        got("x", 2, flow, 1 - flow)
    compute(0, (9, 2, 2))
    for flow in (0, 1):
        got("y", 1, flow, 1 - flow)
    for dy in (1, 3):
        send("c", 1, dy, 0)
        send("c", 1, dy, 1)
    for flow in (0, 1):
        got("xf", 2, flow)
    compute(0, (10, 2, 2))
    half_ready(1, (0, 1, 3))
    compute(1, (0, 1, 6))
    for flow in (0, 1):
        got("x", 3, flow, flow)
        send("xf", 3, flow)
    for flow in (0, 1):
        got("yf", 1, flow)
        send("c", 1, 2, flow)
    compute(1, (6, 1, 7))
    half_ready(1, (2,))
    compute(2, (0, 1, 13))
    for flow in (0, 1):
        got("x", 3, flow, 1 - flow)
    for group in range(3):
        compute(group, (13, 2, 2))
    for flow in (0, 1):
        got("xf", 3, flow)
    for group in range(3):
        compute(group, (14, 2, 1))

    for copy in started:
        copy.wait_send()


def products(low, amplitudes, integrals, side_of, occ_energy, vir_energy):
    anywhere = pl.BlockSpec(memory_space=pl.ANY)
    vmem = pl.BlockSpec(memory_space=pltpu.VMEM)
    pairs = len(KEYS)
    return pl.pallas_call(
        exchange,
        out_shape=pltpu.VMEM((CELLS + 8, BLOCK, BLOCK), jnp.bfloat16),
        in_specs=[pl.BlockSpec(memory_space=pltpu.SMEM), anywhere, anywhere, vmem, anywhere, anywhere],
        out_specs=vmem,
        scratch_shapes=[
            pltpu.VMEM((UNITS, 2, 2, BLOCK, DEPTH), jnp.bfloat16),
            pltpu.VMEM((8, 2, 2, BLOCK, DEPTH), jnp.bfloat16),
            pltpu.VMEM((6, 2, 2, BLOCK, DEPTH), jnp.bfloat16),
            pltpu.VMEM((2, 2, 2, BLOCK, DEPTH), jnp.bfloat16),
            pltpu.VMEM((32, BLOCK, BLOCK), jnp.float32),
            pltpu.VMEM(vir_energy.shape, jnp.float32),
            pltpu.SMEM(occ_energy.shape, jnp.float32),
            pltpu.SemaphoreType.DMA((8,)),
            pltpu.SemaphoreType.DMA((pairs,)),
            pltpu.SemaphoreType.DMA((pairs,)),
        ],
        compiler_params=pltpu.CompilerParams(
            collective_id=0, has_side_effects=True, vmem_limit_bytes=LIMIT
        ),
        name="exchange",
    )(low, amplitudes, integrals, side_of, occ_energy, vir_energy)


def ordered(ranks, dense, out, sem):
    def put(src, slot):
        pltpu.make_async_copy(dense.at[src], out.at[0, 0, slot], sem.at[0]).start()

    def some(t, carry):
        for i in range(8):
            at = t * 8 + i
            rank = ranks[at]

            @pl.when(rank > 0)
            def _():
                put(at, rank - 1)

        return carry

    lax.fori_loop(0, CELLS // 8, some, 0)

    def rest(slot, carry):
        put(CELLS, slot)
        return carry

    lax.fori_loop(ranks[CELLS], TILES, rest, 0)
    whole = dense.at[pl.ds(0, TILES)]
    pltpu.make_async_copy(whole, out.at[0, 0], sem.at[0]).wait()


def in_order(ranks, dense):
    anywhere = pl.BlockSpec(memory_space=pl.ANY)
    return pl.pallas_call(
        ordered,
        out_shape=jax.ShapeDtypeStruct((1, 1, TILES, BLOCK, BLOCK), jnp.bfloat16),
        in_specs=[pl.BlockSpec(memory_space=pltpu.SMEM), anywhere],
        out_specs=anywhere,
        scratch_shapes=[pltpu.SemaphoreType.DMA((1,))],
        compiler_params=pltpu.CompilerParams(vmem_limit_bytes=1024 * 1024),
        name="ordered",
    )(ranks, dense)


def shards(amplitudes, integrals, block_mask, occ_energy, vir_energy):
    col = lax.axis_index("col")
    cell = lax.dynamic_index_in_dim(block_mask.reshape(32, GRID, GRID, 2), col, 2, keepdims=False)
    four = cell.reshape(GRID, 2, GRID, 2)
    low = jnp.sum(four[:, 1], axis=2).T.reshape(CELLS)
    right = jnp.sum(four[..., 1], axis=1).T
    side_of = jnp.broadcast_to(right.astype(jnp.float32).reshape(CELLS, 1, 1), (CELLS, 1, BLOCK))
    flat = cell.reshape(32, 32).astype(jnp.float32)
    at = jnp.arange(32)
    inside = flat @ (at[:, None] <= at[None, :]).astype(jnp.float32)
    ahead = (at[None, :] < at[:, None]).astype(jnp.float32) @ inside[:, 31:]
    upto = inside + ahead
    ranks = jnp.sum((flat * upto).reshape(GRID, 2, GRID, 2), axis=(1, 3)).T.reshape(CELLS)
    ranks = jnp.concatenate([ranks, jnp.broadcast_to(upto[31, 31:], (CELLS,))]).astype(jnp.int32)
    dense = products(
        low,
        amplitudes.reshape(2, BLOCK, DEPTH),
        integrals.reshape(2, BLOCK, DEPTH),
        side_of,
        occ_energy,
        vir_energy.reshape(8, BLOCK),
    )
    return in_order(ranks, dense)


def solution(mesh):
    in_specs = (P(("row", "col"), None), P(("row", "col"), None), P("row", None), P(), P())
    out_specs = P("row", "col", None, None, None)
    return jax.shard_map(shards, mesh=mesh, in_specs=in_specs, out_specs=out_specs, check_vma=False)
```

```python
import functools

import jax
import jax.numpy as jnp
from jax import lax
from jax.experimental import pallas as pl
from jax.experimental.pallas import tpu as pltpu
from jax.sharding import PartitionSpec as P

BLOCK = 128
UNIT = 256
DEPTH = 768
TILES = 192
GRID = 16
CELLS = GRID * GRID
MESH = pl.DeviceIdType.MESH

OWN = 6
CROSS = 7
UNITS = 19
LIMIT = 46 * 1024 * 1024


def table(at, values):
    out = jnp.int32(values[0])
    for i in range(1, len(values)):
        out = jnp.where(at == i, jnp.int32(values[i]), out)
    return out


def names():
    keys = []
    for flow in (0, 1):
        for dist in (1, 2, 3):
            for piece in (0, 1):
                keys.append(("z", flow, dist, piece))
        keys.append(("z", flow, 4, flow))
    for k in range(4):
        for flow in (0, 1):
            for piece in (0, 1):
                keys.append(("x", k, flow, piece))
            keys.append(("xf", k, flow))
    for h in (0, 1):
        for flow in (0, 1):
            for piece in (0, 1):
                keys.append(("y", h, flow, piece))
            keys.append(("yf", h, flow))
        for dy in range(4):
            for piece in (0, 1):
                keys.append(("c", h, dy, piece))
    for flow in (0, 1):
        for dist in (1, 2, 3):
            for piece in (0, 1):
                keys.append(("w", flow, dist, piece))
    return {key: i for i, key in enumerate(keys)}


KEYS = names()
LINES = ((0, 1, 2, 3), (1, 0, 2, 3), (2, 3, 1, 0), (3, 2, 1, 0))


def exchange(
    low_s, amp, ints, side_of, occ, vir_all, dense,
    store, near, far, last, gaps, vir, occ_s,
    local_sem, send_sem, recv_sem,
):
    row, col = lax.axis_index("row"), lax.axis_index("col")
    zl, x = row // 4, row % 4
    zh, y, core = col // 8, (col // 2) % 4, col % 2
    z = zh * 4 + zl

    def at_x(step):
        return (zl * 4 + (x + step) % 4, col)

    def at_y(step):
        return (row, zh * 8 + ((y + step) % 4) * 2 + core)

    def at_z(step):
        there = (z + step) % 8
        return ((there % 4) * 4 + x, (there // 4) * 8 + y * 2 + core)

    partner = (row, zh * 8 + y * 2 + (1 - core))
    step_of = (1, 3)
    ring_of = (1, 7)

    own_copies = []
    for piece, src in enumerate((amp, ints)):
        own_copies.append(pltpu.make_async_copy(src, near.at[0, piece], local_sem.at[piece]))
        own_copies.append(pltpu.make_async_copy(src, store.at[OWN, piece], local_sem.at[2 + piece]))
    for copy in own_copies:
        copy.start()
    occ_copy = pltpu.make_async_copy(occ, occ_s, local_sem.at[5])
    occ_copy.start()
    vir_copy = pltpu.make_async_copy(vir_all, vir, local_sem.at[7])
    vir_copy.start()

    barrier = pltpu.get_barrier_semaphore()
    for there in (at_x(1), at_x(3), at_y(1), at_y(3), at_z(1), at_z(7), partner):
        pl.semaphore_signal(barrier, inc=1, device_id=there, device_id_type=MESH)
    pl.semaphore_wait(barrier, 7)
    for copy in (*own_copies, vir_copy):
        copy.wait()

    slot_k = [OWN] + [table(zl, v) for v in ((3, 0, 3, 0), (4, 3, 0, 1), (5, 4, 1, 2))]
    line_k = [zl] + [table(zl, [lines[k] for lines in LINES]) for k in (1, 2, 3)]

    def rows_at(h, dy, dc, piece):
        if h == 0:
            return near.at[dy * 2 + dc, piece]
        return last.at[dc, piece] if dy == 2 else far.at[(0, 1, 0, 2)[dy] * 2 + dc, piece]

    def line_slot(flow, dist, ahead):
        step = -1 if flow else 1
        slots = []
        for at in range(4):
            there = at + step * ahead
            line = there - step * dist
            slots.append(LINES[there].index(line) if 0 <= there < 4 and 0 <= line < 4 else 0)
        return table(zl, slots)

    def passes_on(flow, dist):
        return (zl >= dist - 1) & (zl <= 2) if flow == 0 else (zl <= 4 - dist) & (zl >= 1)

    def takes(flow, dist):
        return zl >= dist if flow == 0 else zl <= 3 - dist

    started = []
    on_line = []

    def descriptor(key):
        i = KEYS[key]
        kind = key[0]
        if kind == "z":
            _, flow, dist, piece = key
            src = rows_at(0, 0, 0, piece) if dist == 1 else store.at[flow * 3 + dist - 2, piece]
            dst = rows_at(1, 0, 0, piece) if dist == 4 else store.at[flow * 3 + dist - 1, piece]
            there = at_z(ring_of[flow])
        elif kind == "x":
            _, k, flow, piece = key
            src = store.at[slot_k[k], piece]
            dst = store.at[CROSS + (2 if flow == 0 else 0) * 4 + k, piece]
            there = at_x(step_of[flow])
        elif kind == "xf":
            _, k, flow = key
            src = store.at[CROSS + (2 if flow == 0 else 0) * 4 + k, flow]
            dst = store.at[CROSS + 1 * 4 + k, flow]
            if k > 0:
                src, dst = src.at[0], dst.at[0]
            there = at_x(step_of[flow])
        elif kind == "w":
            _, flow, dist, piece = key
            src = store.at[CROSS + 4 + line_slot(flow, dist - 1, 0), piece, 1]
            dst = store.at[CROSS + 4 + line_slot(flow, dist, 1), piece, 1]
            there = at_z(ring_of[flow])
        elif kind == "y":
            _, h, flow, piece = key
            src = rows_at(h, 0, 0, piece)
            dst = rows_at(h, 3 if flow == 0 else 1, 0, piece)
            there = at_y(step_of[flow])
        elif kind == "yf":
            _, h, flow = key
            src = rows_at(h, 3 if flow == 0 else 1, 0, flow)
            dst = rows_at(h, 2, 0, flow)
            there = at_y(step_of[flow])
        else:
            _, h, dy, piece = key
            src = rows_at(h, dy, 0, piece)
            dst = rows_at(h, dy, 1, piece)
            there = partner
        return pltpu.make_async_remote_copy(
            src_ref=src,
            dst_ref=dst,
            send_sem=send_sem.at[i],
            recv_sem=recv_sem.at[i],
            device_id=there,
            device_id_type=MESH,
        )

    def send(*key):
        copy = descriptor(key)
        copy.start()
        started.append(copy)

    def got(*key):
        descriptor(key).wait_recv()

    def send_line(dist):
        for flow in (0, 1):

            @pl.when(passes_on(flow, dist))
            def _(flow=flow):
                for piece in (0, 1):
                    descriptor(("w", flow, dist, piece)).start()

            on_line.append((flow, dist))

    def got_line(dist):
        for flow in (0, 1):

            @pl.when(takes(flow, dist))
            def _(flow=flow):
                for piece in (0, 1):
                    descriptor(("w", flow, dist, piece)).wait_recv()

    def send_unit(kind, at):
        for i in (0, 1):
            send(kind, at, 0, i)
            send(kind, at, 1, 1 - i)

    groups = (
        (near, 0, [(dy, dc) for dy in range(4) for dc in (0, 1)]),
        (far, 1, [(dy, dc) for dy in (0, 1, 3) for dc in (0, 1)]),
        (last, 1, [(2, dc) for dc in (0, 1)]),
    )
    first_line = vir[pl.ds((2 * col) % 8, 1), :]
    second_line = vir[pl.ds((2 * col + 1) % 8, 1), :]

    def chunk(group, k, dx):
        rows_ref, half, members = groups[group]
        unit = slot_k[k] if dx == 0 else CROSS + (dx - 1) * 4 + k
        there = line_k[k] * 4 + (x + dx) % 4
        side = zh if half == 0 else 1 - zh
        places = [((y + dy) % 4) * 2 + (core + dc) % 2 for dy, dc in members]
        ats = [there * GRID + side * 8 + p for p in places]
        lows = [low_s[at] for at in ats]
        dims = (((1,), (1,)), ((), ()))
        both = [
            lax.dot_general(
                jnp.concatenate([rows_ref[i, piece, low] for i, low in enumerate(lows)], axis=0),
                store[unit, 1 - piece].reshape(UNIT, DEPTH),
                dims,
                preferred_element_type=jnp.float32,
            )
            for piece in (0, 1)
        ]
        both = both[0] + both[1]
        level = occ_s[there * 4 + col // 4]
        for i, (place, at) in enumerate(zip(places, ats)):
            mine = both[i * BLOCK : (i + 1) * BLOCK]
            right = side_of[at]
            across = jnp.where(right > 0.5, second_line, first_line) - level
            kept = jnp.where(jnp.broadcast_to(right, (BLOCK, BLOCK)) > 0.5, mine[:, BLOCK:], mine[:, :BLOCK])
            below = gaps[(side * 8 + place) * 2 + lows[i]] + across
            dense[at] = (kept / below).astype(jnp.bfloat16)

    def compute(group, *todo):
        for first, step, count in todo:
            for at in range(first, first + step * count, step):
                chunk(group, at // 4, at % 4)

    def half_ready(h, dys):
        for dy in dys:
            for piece in (0, 1):
                got("c", h, dy, piece)

    for i in (0, 1):
        send("z", 0, 1, i)
        send("z", 1, 1, 1 - i)
        send("x", 0, 0, i)
        send("x", 0, 1, 1 - i)
        send("y", 0, 0, i)
        send("y", 0, 1, 1 - i)
    send("c", 0, 0, 0)
    send("c", 0, 0, 1)
    occ_copy.wait()
    for j in range(8):
        turned = jnp.broadcast_to(vir[j : j + 1, :], (BLOCK, BLOCK)).T
        for t in range(4):
            gaps[j + 8 * t] = turned - occ_s[row * 4 + t]
    dense[CELLS] = jnp.zeros((BLOCK, BLOCK), jnp.bfloat16)
    for flow in (0, 1):
        got("z", flow, 1, flow)
        send("z", flow, 2, flow)
        got("x", 0, flow, flow)
        send("xf", 0, flow)
        got("y", 0, flow, flow)
        send("yf", 0, flow)
    for flow in (0, 1):
        got("z", flow, 1, 1 - flow)
    send_unit("x", 1)
    for flow in (0, 1):
        got("y", 0, flow, 1 - flow)
    for dy in (1, 3):
        send("c", 0, dy, 0)
        send("c", 0, dy, 1)
    for flow in (0, 1):
        got("z", flow, 2, flow)
        send("z", flow, 3, flow)
        send("z", flow, 2, 1 - flow)
    for flow in (0, 1):
        got("yf", 0, flow)
        send("c", 0, 2, flow)
    half_ready(0, range(4))
    compute(0, (0, 1, 1))
    for flow in (0, 1):
        got("z", flow, 3, flow)
        send("z", flow, 4, flow)
    for flow in (0, 1):
        got("x", 0, flow, 1 - flow)
        got("x", 1, flow, flow)
        send("xf", 1, flow)
    compute(0, (1, 2, 2))
    for flow in (0, 1):
        got("z", flow, 2, 1 - flow)
        send("z", flow, 3, 1 - flow)
    send_unit("x", 2)
    for flow in (0, 1):
        got("xf", 0, flow)
    send_line(1)
    compute(0, (2, 2, 2))
    for flow in (0, 1):
        got("x", 1, flow, 1 - flow)
    compute(0, (5, 2, 2))
    for flow in (0, 1):
        got("z", flow, 4, flow)
    send_unit("y", 1)
    send("c", 1, 0, 0)
    send("c", 1, 0, 1)
    for flow in (0, 1):
        got("x", 2, flow, flow)
        send("xf", 2, flow)
    compute(0, (8, 1, 1))
    for flow in (0, 1):
        got("z", flow, 3, 1 - flow)
    send_unit("x", 3)
    for flow in (0, 1):
        got("y", 1, flow, flow)
        send("yf", 1, flow)
    for flow in (0, 1):
        got("x", 2, flow, 1 - flow)
    compute(0, (9, 2, 2))
    for flow in (0, 1):
        got("y", 1, flow, 1 - flow)
    for dy in (1, 3):
        send("c", 1, dy, 0)
        send("c", 1, dy, 1)
    got_line(1)
    send_line(2)
    for flow in (0, 1):
        got("xf", 1, flow)
    compute(0, (6, 6, 2))
    half_ready(1, (0, 1, 3))
    compute(1, (0, 1, 6))
    for flow in (0, 1):
        got("x", 3, flow, flow)
        send("xf", 3, flow)
    for flow in (0, 1):
        got("yf", 1, flow)
        send("c", 1, 2, flow)
    got_line(2)
    send_line(3)
    for flow in (0, 1):
        got("xf", 2, flow)
    compute(0, (10, 1, 1))
    compute(1, (6, 1, 7))
    half_ready(1, (2,))
    compute(2, (0, 1, 13))
    for flow in (0, 1):
        got("x", 3, flow, 1 - flow)
    for group in range(3):
        compute(group, (13, 2, 2))
    for flow in (0, 1):
        got("xf", 3, flow)
    got_line(3)
    for group in range(3):
        compute(group, (14, 2, 1))

    for copy in started:
        copy.wait_send()
    for flow, dist in on_line:

        @pl.when(passes_on(flow, dist))
        def _(flow=flow, dist=dist):
            for piece in (0, 1):
                descriptor(("w", flow, dist, piece)).wait_send()


def products(low, amplitudes, integrals, side_of, occ_energy, vir_energy):
    anywhere = pl.BlockSpec(memory_space=pl.ANY)
    vmem = pl.BlockSpec(memory_space=pltpu.VMEM)
    pairs = len(KEYS)
    return pl.pallas_call(
        exchange,
        out_shape=pltpu.VMEM((CELLS + 8, BLOCK, BLOCK), jnp.bfloat16),
        in_specs=[pl.BlockSpec(memory_space=pltpu.SMEM), anywhere, anywhere, vmem, anywhere, anywhere],
        out_specs=vmem,
        scratch_shapes=[
            pltpu.VMEM((UNITS, 2, 2, BLOCK, DEPTH), jnp.bfloat16),
            pltpu.VMEM((8, 2, 2, BLOCK, DEPTH), jnp.bfloat16),
            pltpu.VMEM((6, 2, 2, BLOCK, DEPTH), jnp.bfloat16),
            pltpu.VMEM((2, 2, 2, BLOCK, DEPTH), jnp.bfloat16),
            pltpu.VMEM((32, BLOCK, BLOCK), jnp.float32),
            pltpu.VMEM(vir_energy.shape, jnp.float32),
            pltpu.SMEM(occ_energy.shape, jnp.float32),
            pltpu.SemaphoreType.DMA((8,)),
            pltpu.SemaphoreType.DMA((pairs,)),
            pltpu.SemaphoreType.DMA((pairs,)),
        ],
        compiler_params=pltpu.CompilerParams(
            collective_id=0, has_side_effects=True, vmem_limit_bytes=LIMIT
        ),
        name="exchange",
    )(low, amplitudes, integrals, side_of, occ_energy, vir_energy)


def ordered(ranks, dense, out, sem):
    def put(src, slot):
        pltpu.make_async_copy(dense.at[src], out.at[0, 0, slot], sem.at[0]).start()

    def some(t, carry):
        for i in range(8):
            at = t * 8 + i
            rank = ranks[at]

            @pl.when(rank > 0)
            def _():
                put(at, rank - 1)

        return carry

    lax.fori_loop(0, CELLS // 8, some, 0)

    def rest(slot, carry):
        put(CELLS, slot)
        return carry

    lax.fori_loop(ranks[CELLS], TILES, rest, 0)
    whole = dense.at[pl.ds(0, TILES)]
    pltpu.make_async_copy(whole, out.at[0, 0], sem.at[0]).wait()


def in_order(ranks, dense):
    anywhere = pl.BlockSpec(memory_space=pl.ANY)
    return pl.pallas_call(
        ordered,
        out_shape=jax.ShapeDtypeStruct((1, 1, TILES, BLOCK, BLOCK), jnp.bfloat16),
        in_specs=[pl.BlockSpec(memory_space=pltpu.SMEM), anywhere],
        out_specs=anywhere,
        scratch_shapes=[pltpu.SemaphoreType.DMA((1,))],
        compiler_params=pltpu.CompilerParams(vmem_limit_bytes=1024 * 1024),
        name="ordered",
    )(ranks, dense)


def shards(amplitudes, integrals, block_mask, occ_energy, vir_energy):
    col = lax.axis_index("col")
    cell = lax.dynamic_index_in_dim(block_mask.reshape(32, GRID, GRID, 2), col, 2, keepdims=False)
    four = cell.reshape(GRID, 2, GRID, 2)
    low = jnp.sum(four[:, 1], axis=2).T.reshape(CELLS)
    right = jnp.sum(four[..., 1], axis=1).T
    side_of = jnp.broadcast_to(right.astype(jnp.float32).reshape(CELLS, 1, 1), (CELLS, 1, BLOCK))
    flat = cell.reshape(32, 32).astype(jnp.float32)
    at = jnp.arange(32)
    inside = flat @ (at[:, None] <= at[None, :]).astype(jnp.float32)
    ahead = (at[None, :] < at[:, None]).astype(jnp.float32) @ inside[:, 31:]
    upto = inside + ahead
    ranks = jnp.sum((flat * upto).reshape(GRID, 2, GRID, 2), axis=(1, 3)).T.reshape(CELLS)
    ranks = jnp.concatenate([ranks, jnp.broadcast_to(upto[31, 31:], (CELLS,))]).astype(jnp.int32)
    dense = products(
        low,
        amplitudes.reshape(2, BLOCK, DEPTH),
        integrals.reshape(2, BLOCK, DEPTH),
        side_of,
        occ_energy,
        vir_energy.reshape(8, BLOCK),
    )
    return in_order(ranks, dense)


def solution(mesh):
    in_specs = (P(("row", "col"), None), P(("row", "col"), None), P("row", None), P(), P())
    out_specs = P("row", "col", None, None, None)
    return jax.shard_map(shards, mesh=mesh, in_specs=in_specs, out_specs=out_specs, check_vma=False)
```

```python
import functools

import jax
import jax.numpy as jnp
from jax import lax
from jax.experimental import pallas as pl
from jax.experimental.pallas import tpu as pltpu
from jax.sharding import PartitionSpec as P

BLOCK = 128
UNIT = 256
DEPTH = 768
TILES = 192
GRID = 16
CELLS = GRID * GRID
MESH = pl.DeviceIdType.MESH

OWN = 6
CROSS = 7
UNITS = 19
LIMIT = 46 * 1024 * 1024


def table(at, values):
    out = jnp.int32(values[0])
    for i in range(1, len(values)):
        out = jnp.where(at == i, jnp.int32(values[i]), out)
    return out


def names():
    keys = []
    for flow in (0, 1):
        for dist in (1, 2, 3):
            for piece in (0, 1):
                keys.append(("z", flow, dist, piece))
        keys.append(("z", flow, 4, flow))
    for k in range(4):
        for flow in (0, 1):
            for piece in (0, 1):
                keys.append(("x", k, flow, piece))
            keys.append(("xf", k, flow))
    for h in (0, 1):
        for flow in (0, 1):
            for piece in (0, 1):
                keys.append(("y", h, flow, piece))
            keys.append(("yf", h, flow))
        for dy in range(4):
            for piece in (0, 1):
                keys.append(("c", h, dy, piece))
    for flow in (0, 1):
        for dist in (1, 2, 3):
            for piece in (0, 1):
                keys.append(("w", flow, dist, piece))
    return {key: i for i, key in enumerate(keys)}


KEYS = names()
LINES = ((0, 1, 2, 3), (1, 0, 2, 3), (2, 3, 1, 0), (3, 2, 1, 0))


def exchange(
    sides, amp, ints, occ, vir_all, dense,
    store, near, far, last, gaps, vir, occ_s,
    local_sem, send_sem, recv_sem,
):
    row, col = lax.axis_index("row"), lax.axis_index("col")
    zl, x = row // 4, row % 4
    zh, y, core = col // 8, (col // 2) % 4, col % 2
    z = zh * 4 + zl

    def at_x(step):
        return (zl * 4 + (x + step) % 4, col)

    def at_y(step):
        return (row, zh * 8 + ((y + step) % 4) * 2 + core)

    def at_z(step):
        there = (z + step) % 8
        return ((there % 4) * 4 + x, (there // 4) * 8 + y * 2 + core)

    partner = (row, zh * 8 + y * 2 + (1 - core))
    step_of = (1, 3)
    ring_of = (1, 7)

    own_copies = []
    for piece, src in enumerate((amp, ints)):
        own_copies.append(pltpu.make_async_copy(src, near.at[0, piece], local_sem.at[piece]))
        own_copies.append(pltpu.make_async_copy(src, store.at[OWN, piece], local_sem.at[2 + piece]))
    for copy in own_copies:
        copy.start()
    occ_copy = pltpu.make_async_copy(occ, occ_s, local_sem.at[5])
    occ_copy.start()
    vir_copy = pltpu.make_async_copy(vir_all, vir, local_sem.at[7])
    vir_copy.start()

    barrier = pltpu.get_barrier_semaphore()
    for there in (at_x(1), at_x(3), at_y(1), at_y(3), at_z(1), at_z(7), partner):
        pl.semaphore_signal(barrier, inc=1, device_id=there, device_id_type=MESH)
    pl.semaphore_wait(barrier, 7)
    for copy in (*own_copies, vir_copy):
        copy.wait()

    slot_k = [OWN] + [table(zl, v) for v in ((3, 0, 3, 0), (4, 3, 0, 1), (5, 4, 1, 2))]
    line_k = [zl] + [table(zl, [lines[k] for lines in LINES]) for k in (1, 2, 3)]

    def rows_at(h, dy, dc, piece):
        if h == 0:
            return near.at[dy * 2 + dc, piece]
        return last.at[dc, piece] if dy == 2 else far.at[(0, 1, 0, 2)[dy] * 2 + dc, piece]

    def line_slot(flow, dist, ahead):
        step = -1 if flow else 1
        slots = []
        for at in range(4):
            there = at + step * ahead
            line = there - step * dist
            slots.append(LINES[there].index(line) if 0 <= there < 4 and 0 <= line < 4 else 0)
        return table(zl, slots)

    def passes_on(flow, dist):
        return (zl >= dist - 1) & (zl <= 2) if flow == 0 else (zl <= 4 - dist) & (zl >= 1)

    def takes(flow, dist):
        return zl >= dist if flow == 0 else zl <= 3 - dist

    started = []
    on_line = []

    def descriptor(key):
        i = KEYS[key]
        kind = key[0]
        if kind == "z":
            _, flow, dist, piece = key
            src = rows_at(0, 0, 0, piece) if dist == 1 else store.at[flow * 3 + dist - 2, piece]
            dst = rows_at(1, 0, 0, piece) if dist == 4 else store.at[flow * 3 + dist - 1, piece]
            there = at_z(ring_of[flow])
        elif kind == "x":
            _, k, flow, piece = key
            src = store.at[slot_k[k], piece]
            dst = store.at[CROSS + (2 if flow == 0 else 0) * 4 + k, piece]
            there = at_x(step_of[flow])
        elif kind == "xf":
            _, k, flow = key
            src = store.at[CROSS + (2 if flow == 0 else 0) * 4 + k, flow]
            dst = store.at[CROSS + 1 * 4 + k, flow]
            if k > 0:
                src, dst = src.at[0], dst.at[0]
            there = at_x(step_of[flow])
        elif kind == "w":
            _, flow, dist, piece = key
            src = store.at[CROSS + 4 + line_slot(flow, dist - 1, 0), piece, 1]
            dst = store.at[CROSS + 4 + line_slot(flow, dist, 1), piece, 1]
            there = at_z(ring_of[flow])
        elif kind == "y":
            _, h, flow, piece = key
            src = rows_at(h, 0, 0, piece)
            dst = rows_at(h, 3 if flow == 0 else 1, 0, piece)
            there = at_y(step_of[flow])
        elif kind == "yf":
            _, h, flow = key
            src = rows_at(h, 3 if flow == 0 else 1, 0, flow)
            dst = rows_at(h, 2, 0, flow)
            there = at_y(step_of[flow])
        else:
            _, h, dy, piece = key
            src = rows_at(h, dy, 0, piece)
            dst = rows_at(h, dy, 1, piece)
            there = partner
        return pltpu.make_async_remote_copy(
            src_ref=src,
            dst_ref=dst,
            send_sem=send_sem.at[i],
            recv_sem=recv_sem.at[i],
            device_id=there,
            device_id_type=MESH,
        )

    def send(*key):
        copy = descriptor(key)
        copy.start()
        started.append(copy)

    def got(*key):
        descriptor(key).wait_recv()

    def send_line(dist):
        for flow in (0, 1):

            @pl.when(passes_on(flow, dist))
            def _(flow=flow):
                for piece in (0, 1):
                    descriptor(("w", flow, dist, piece)).start()

            on_line.append((flow, dist))

    def got_line(dist):
        for flow in (0, 1):

            @pl.when(takes(flow, dist))
            def _(flow=flow):
                for piece in (0, 1):
                    descriptor(("w", flow, dist, piece)).wait_recv()

    def send_unit(kind, at):
        for i in (0, 1):
            send(kind, at, 0, i)
            send(kind, at, 1, 1 - i)

    groups = (
        (near, 0, [(dy, dc) for dy in range(4) for dc in (0, 1)]),
        (far, 1, [(dy, dc) for dy in (0, 1, 3) for dc in (0, 1)]),
        (last, 1, [(2, dc) for dc in (0, 1)]),
    )
    first_line = vir[pl.ds((2 * col) % 8, 1), :]
    second_line = vir[pl.ds((2 * col + 1) % 8, 1), :]

    def chunk(group, k, dx):
        rows_ref, half, members = groups[group]
        unit = slot_k[k] if dx == 0 else CROSS + (dx - 1) * 4 + k
        there = line_k[k] * 4 + (x + dx) % 4
        side = zh if half == 0 else 1 - zh
        uppers = [side * 8 + ((y + dy) % 4) * 2 + (core + dc) % 2 for dy, dc in members]
        lows = [sides[there, upper] for upper in uppers]
        dims = (((1,), (1,)), ((), ()))
        both = [
            lax.dot_general(
                jnp.concatenate([rows_ref[i, piece, low] for i, low in enumerate(lows)], axis=0),
                store[unit, 1 - piece].reshape(UNIT, DEPTH),
                dims,
                preferred_element_type=jnp.float32,
            )
            for piece in (0, 1)
        ]
        both = both[0] + both[1]
        level = occ_s[there * 4 + col // 4]
        for i, upper in enumerate(uppers):
            mine = both[i * BLOCK : (i + 1) * BLOCK]
            right = jnp.full((1, BLOCK), sides[GRID + there, GRID + upper])
            across = jnp.where(right > 0, second_line, first_line) - level
            kept = jnp.where(jnp.broadcast_to(right, (BLOCK, BLOCK)) > 0, mine[:, BLOCK:], mine[:, :BLOCK])
            below = gaps[upper * 2 + lows[i]] + across
            dense[there * GRID + upper] = (kept / below).astype(jnp.bfloat16)

    def compute(group, *todo):
        for first, step, count in todo:
            for at in range(first, first + step * count, step):
                chunk(group, at // 4, at % 4)

    def half_ready(h, dys):
        for dy in dys:
            for piece in (0, 1):
                got("c", h, dy, piece)

    for i in (0, 1):
        send("z", 0, 1, i)
        send("z", 1, 1, 1 - i)
        send("x", 0, 0, i)
        send("x", 0, 1, 1 - i)
        send("y", 0, 0, i)
        send("y", 0, 1, 1 - i)
    send("c", 0, 0, 0)
    send("c", 0, 0, 1)
    occ_copy.wait()
    for j in range(8):
        turned = jnp.broadcast_to(vir[j : j + 1, :], (BLOCK, BLOCK)).T
        for t in range(4):
            gaps[j + 8 * t] = turned - occ_s[row * 4 + t]
    dense[CELLS] = jnp.zeros((BLOCK, BLOCK), jnp.bfloat16)
    for flow in (0, 1):
        got("z", flow, 1, flow)
        send("z", flow, 2, flow)
        got("x", 0, flow, flow)
        send("xf", 0, flow)
        got("y", 0, flow, flow)
        send("yf", 0, flow)
    for flow in (0, 1):
        got("z", flow, 1, 1 - flow)
    send_unit("x", 1)
    for flow in (0, 1):
        got("y", 0, flow, 1 - flow)
    for dy in (1, 3):
        send("c", 0, dy, 0)
        send("c", 0, dy, 1)
    for flow in (0, 1):
        got("z", flow, 2, flow)
        send("z", flow, 3, flow)
        send("z", flow, 2, 1 - flow)
    for flow in (0, 1):
        got("yf", 0, flow)
        send("c", 0, 2, flow)
    half_ready(0, range(4))
    compute(0, (0, 1, 1))
    for flow in (0, 1):
        got("z", flow, 3, flow)
        send("z", flow, 4, flow)
    for flow in (0, 1):
        got("x", 0, flow, 1 - flow)
        got("x", 1, flow, flow)
        send("xf", 1, flow)
    compute(0, (1, 2, 2))
    for flow in (0, 1):
        got("z", flow, 2, 1 - flow)
        send("z", flow, 3, 1 - flow)
    send_unit("x", 2)
    for flow in (0, 1):
        got("xf", 0, flow)
    send_line(1)
    compute(0, (2, 2, 2))
    for flow in (0, 1):
        got("x", 1, flow, 1 - flow)
    compute(0, (5, 2, 2))
    for flow in (0, 1):
        got("z", flow, 4, flow)
    send_unit("y", 1)
    send("c", 1, 0, 0)
    send("c", 1, 0, 1)
    for flow in (0, 1):
        got("x", 2, flow, flow)
        send("xf", 2, flow)
    compute(0, (8, 1, 1))
    for flow in (0, 1):
        got("z", flow, 3, 1 - flow)
    send_unit("x", 3)
    for flow in (0, 1):
        got("y", 1, flow, flow)
        send("yf", 1, flow)
    for flow in (0, 1):
        got("x", 2, flow, 1 - flow)
    compute(0, (9, 2, 2), (12, 1, 1))
    for flow in (0, 1):
        got("y", 1, flow, 1 - flow)
    for dy in (1, 3):
        send("c", 1, dy, 0)
        send("c", 1, dy, 1)
    got_line(1)
    send_line(2)
    for flow in (0, 1):
        got("xf", 1, flow)
    compute(0, (6, 1, 1))
    half_ready(1, (0, 1, 3))
    compute(1, (0, 1, 10))
    for flow in (0, 1):
        got("x", 3, flow, flow)
        send("xf", 3, flow)
    for flow in (0, 1):
        got("yf", 1, flow)
        send("c", 1, 2, flow)
    got_line(2)
    send_line(3)
    for flow in (0, 1):
        got("xf", 2, flow)
    compute(0, (10, 1, 1))
    compute(1, (10, 1, 3))
    half_ready(1, (2,))
    compute(2, (0, 1, 13))
    for flow in (0, 1):
        got("x", 3, flow, 1 - flow)
    for group in range(3):
        compute(group, (13, 2, 2))
    for flow in (0, 1):
        got("xf", 3, flow)
    got_line(3)
    for group in range(3):
        compute(group, (14, 2, 1))

    for copy in started:
        copy.wait_send()
    for flow, dist in on_line:

        @pl.when(passes_on(flow, dist))
        def _(flow=flow, dist=dist):
            for piece in (0, 1):
                descriptor(("w", flow, dist, piece)).wait_send()


def products(sides, amplitudes, integrals, occ_energy, vir_energy):
    anywhere = pl.BlockSpec(memory_space=pl.ANY)
    vmem = pl.BlockSpec(memory_space=pltpu.VMEM)
    pairs = len(KEYS)
    return pl.pallas_call(
        exchange,
        out_shape=pltpu.VMEM((CELLS + 8, BLOCK, BLOCK), jnp.bfloat16),
        in_specs=[pl.BlockSpec(memory_space=pltpu.SMEM)] + [anywhere] * 4,
        out_specs=vmem,
        scratch_shapes=[
            pltpu.VMEM((UNITS, 2, 2, BLOCK, DEPTH), jnp.bfloat16),
            pltpu.VMEM((8, 2, 2, BLOCK, DEPTH), jnp.bfloat16),
            pltpu.VMEM((6, 2, 2, BLOCK, DEPTH), jnp.bfloat16),
            pltpu.VMEM((2, 2, 2, BLOCK, DEPTH), jnp.bfloat16),
            pltpu.VMEM((32, BLOCK, BLOCK), jnp.float32),
            pltpu.VMEM(vir_energy.shape, jnp.float32),
            pltpu.SMEM(occ_energy.shape, jnp.float32),
            pltpu.SemaphoreType.DMA((8,)),
            pltpu.SemaphoreType.DMA((pairs,)),
            pltpu.SemaphoreType.DMA((pairs,)),
        ],
        compiler_params=pltpu.CompilerParams(
            collective_id=0, has_side_effects=True, vmem_limit_bytes=LIMIT
        ),
        name="exchange",
    )(sides, amplitudes, integrals, occ_energy, vir_energy)


def ordered(ranks, dense, out, sem):
    def put(src, slot):
        pltpu.make_async_copy(dense.at[src], out.at[0, 0, slot], sem.at[0]).start()

    def some(t, count):
        for i in range(GRID):
            rank = ranks[t, i]

            @pl.when(rank > 0)
            def _():
                put(t * GRID + i, rank - 1)

            count = count + jnp.minimum(rank, 1)
        return count

    count = lax.fori_loop(0, GRID, some, jnp.int32(0))

    def rest(slot, carry):
        put(CELLS, slot)
        return carry

    lax.fori_loop(count, TILES, rest, 0)
    whole = dense.at[pl.ds(0, TILES)]
    pltpu.make_async_copy(whole, out.at[0, 0], sem.at[0]).wait()


def in_order(ranks, dense):
    anywhere = pl.BlockSpec(memory_space=pl.ANY)
    return pl.pallas_call(
        ordered,
        out_shape=jax.ShapeDtypeStruct((1, 1, TILES, BLOCK, BLOCK), jnp.bfloat16),
        in_specs=[pl.BlockSpec(memory_space=pltpu.SMEM), anywhere],
        out_specs=anywhere,
        scratch_shapes=[pltpu.SemaphoreType.DMA((1,))],
        compiler_params=pltpu.CompilerParams(vmem_limit_bytes=1024 * 1024),
        name="ordered",
    )(ranks, dense)


def shards(amplitudes, integrals, block_mask, occ_energy, vir_energy):
    col = lax.axis_index("col")

    def chosen(shape, test):
        down, across = (lax.broadcasted_iota(jnp.int32, shape, axis) for axis in (0, 1))
        return test(down, across).astype(jnp.float32)

    pick = chosen((32, 512), lambda v, at: at == v // 2 * 32 + 2 * col + v % 2)
    cell = lax.dot_general(pick, block_mask.astype(jnp.float32), (((1,), (1,)), ((), ())))
    rows = chosen((GRID, 32), lambda r, v: v // 2 == r)
    lines = chosen((32, GRID), lambda u, c: u // 2 == c)
    all_rows = chosen((32, 32), lambda r, v: jnp.where(r < GRID, v // 2 == r, v == 2 * (r - GRID) + 1))
    all_lines = chosen((32, 32), lambda u, c: jnp.where(c < GRID, u == 2 * c + 1, u // 2 == c - GRID))
    sides = (all_rows @ (cell @ all_lines)).astype(jnp.int32)
    upto = chosen((32, 32), lambda v, at: at <= v) @ cell
    upto = upto + jnp.sum(cell, axis=0, keepdims=True) @ chosen((32, 32), lambda at, u: at < u)
    ranks = (rows @ ((cell * upto) @ lines)).astype(jnp.int32)
    dense = products(
        sides,
        amplitudes.reshape(2, BLOCK, DEPTH),
        integrals.reshape(2, BLOCK, DEPTH),
        occ_energy,
        vir_energy.reshape(8, BLOCK),
    )
    return in_order(ranks, dense)


def solution(mesh):
    in_specs = (P(("row", "col"), None), P(("row", "col"), None), P("row", None), P(), P())
    out_specs = P("row", "col", None, None, None)
    return jax.shard_map(shards, mesh=mesh, in_specs=in_specs, out_specs=out_specs, check_vma=False)
```

```python
import functools

import jax
import jax.numpy as jnp
from jax import lax
from jax.experimental import pallas as pl
from jax.experimental.pallas import tpu as pltpu
from jax.sharding import PartitionSpec as P

BLOCK = 128
UNIT = 256
DEPTH = 768
TILES = 192
GRID = 16
CELLS = GRID * GRID
MESH = pl.DeviceIdType.MESH

OWN = 6
CROSS = 7
UNITS = 19
LIMIT = 46 * 1024 * 1024


def table(at, values):
    out = jnp.int32(values[0])
    for i in range(1, len(values)):
        out = jnp.where(at == i, jnp.int32(values[i]), out)
    return out


def names():
    keys = []
    for flow in (0, 1):
        for dist in (1, 2, 3):
            for piece in (0, 1):
                keys.append(("z", flow, dist, piece))
        keys.append(("z", flow, 4, flow))
    for k in range(4):
        for flow in (0, 1):
            for piece in (0, 1):
                keys.append(("x", k, flow, piece))
            keys.append(("xf", k, flow))
    for h in (0, 1):
        for flow in (0, 1):
            for piece in (0, 1):
                keys.append(("y", h, flow, piece))
            keys.append(("yf", h, flow))
        for dy in range(4):
            for piece in (0, 1):
                keys.append(("c", h, dy, piece))
    for flow in (0, 1):
        for dist in (1, 2, 3):
            for piece in (0, 1):
                keys.append(("w", flow, dist, piece))
    return {key: i for i, key in enumerate(keys)}


KEYS = names()
LINES = ((0, 1, 2, 3), (1, 0, 2, 3), (2, 3, 1, 0), (3, 2, 1, 0))


def exchange(
    sides, amp, ints, occ, vir_all, dense,
    store, near, far, last, gaps, vir, occ_s,
    local_sem, send_sem, recv_sem,
):
    row, col = lax.axis_index("row"), lax.axis_index("col")
    zl, x = row // 4, row % 4
    zh, y, core = col // 8, (col // 2) % 4, col % 2
    z = zh * 4 + zl

    def at_x(step):
        return (zl * 4 + (x + step) % 4, col)

    def at_y(step):
        return (row, zh * 8 + ((y + step) % 4) * 2 + core)

    def at_z(step):
        there = (z + step) % 8
        return ((there % 4) * 4 + x, (there // 4) * 8 + y * 2 + core)

    partner = (row, zh * 8 + y * 2 + (1 - core))
    step_of = (1, 3)
    ring_of = (1, 7)

    own_copies = []
    for piece, src in enumerate((amp, ints)):
        own_copies.append(pltpu.make_async_copy(src, near.at[0, piece], local_sem.at[piece]))
        own_copies.append(pltpu.make_async_copy(src, store.at[OWN, piece], local_sem.at[2 + piece]))
    for copy in own_copies:
        copy.start()
    occ_copy = pltpu.make_async_copy(occ, occ_s, local_sem.at[5])
    occ_copy.start()
    vir_copy = pltpu.make_async_copy(vir_all, vir, local_sem.at[7])
    vir_copy.start()

    barrier = pltpu.get_barrier_semaphore()
    for there in (at_x(1), at_x(3), at_y(1), at_y(3), at_z(1), at_z(7), partner):
        pl.semaphore_signal(barrier, inc=1, device_id=there, device_id_type=MESH)
    pl.semaphore_wait(barrier, 7)
    for copy in (*own_copies, vir_copy):
        copy.wait()

    slot_k = [OWN] + [table(zl, v) for v in ((3, 0, 3, 0), (4, 3, 0, 1), (5, 4, 1, 2))]
    line_k = [zl] + [table(zl, [lines[k] for lines in LINES]) for k in (1, 2, 3)]

    def rows_at(h, dy, dc, piece):
        if h == 0:
            return near.at[dy * 2 + dc, piece]
        return last.at[dc, piece] if dy == 2 else far.at[(0, 1, 0, 2)[dy] * 2 + dc, piece]

    early = table(zl, (1, 1, 0, 0))

    def line_slot(flow, dist, ahead):
        step = -1 if flow else 1
        slots = []
        for at in range(4):
            there = at + step * ahead
            line = there - step * dist
            slots.append(LINES[there].index(line) if 0 <= there < 4 and 0 <= line < 4 else 0)
        return table(zl, slots)

    def passes_on(flow, dist):
        return (zl >= dist - 1) & (zl <= 2) if flow == 0 else (zl <= 4 - dist) & (zl >= 1)

    def takes(flow, dist):
        return zl >= dist if flow == 0 else zl <= 3 - dist

    started = []
    on_line = []

    def descriptor(key):
        i = KEYS[key]
        kind = key[0]
        if kind == "z":
            _, flow, dist, piece = key
            src = rows_at(0, 0, 0, piece) if dist == 1 else store.at[flow * 3 + dist - 2, piece]
            dst = rows_at(1, 0, 0, piece) if dist == 4 else store.at[flow * 3 + dist - 1, piece]
            there = at_z(ring_of[flow])
        elif kind == "x":
            _, k, flow, piece = key
            if k == 2:
                piece = early if piece == 0 else 1 - early
            src = store.at[slot_k[k], piece]
            dst = store.at[CROSS + (2 if flow == 0 else 0) * 4 + k, piece]
            there = at_x(step_of[flow])
        elif kind == "xf":
            _, k, flow = key
            src = store.at[CROSS + (2 if flow == 0 else 0) * 4 + k, flow]
            dst = store.at[CROSS + 1 * 4 + k, flow]
            if k > 0:
                src, dst = src.at[0], dst.at[0]
            there = at_x(step_of[flow])
        elif kind == "w":
            _, flow, dist, piece = key
            src = store.at[CROSS + 4 + line_slot(flow, dist - 1, 0), piece, 1]
            dst = store.at[CROSS + 4 + line_slot(flow, dist, 1), piece, 1]
            there = at_z(ring_of[flow])
        elif kind == "y":
            _, h, flow, piece = key
            src = rows_at(h, 0, 0, piece)
            dst = rows_at(h, 3 if flow == 0 else 1, 0, piece)
            there = at_y(step_of[flow])
        elif kind == "yf":
            _, h, flow = key
            src = rows_at(h, 3 if flow == 0 else 1, 0, flow)
            dst = rows_at(h, 2, 0, flow)
            there = at_y(step_of[flow])
        else:
            _, h, dy, piece = key
            src = rows_at(h, dy, 0, piece)
            dst = rows_at(h, dy, 1, piece)
            there = partner
        return pltpu.make_async_remote_copy(
            src_ref=src,
            dst_ref=dst,
            send_sem=send_sem.at[i],
            recv_sem=recv_sem.at[i],
            device_id=there,
            device_id_type=MESH,
        )

    def send(*key):
        copy = descriptor(key)
        copy.start()
        started.append(copy)

    def got(*key):
        descriptor(key).wait_recv()

    def send_line(dist):
        for flow in (0, 1):

            @pl.when(passes_on(flow, dist))
            def _(flow=flow):
                for piece in (0, 1):
                    descriptor(("w", flow, dist, piece)).start()

            on_line.append((flow, dist))

    def got_line(dist):
        for flow in (0, 1):

            @pl.when(takes(flow, dist))
            def _(flow=flow):
                for piece in (0, 1):
                    descriptor(("w", flow, dist, piece)).wait_recv()

    def send_unit(kind, at):
        for i in (0, 1):
            send(kind, at, 0, i)
            send(kind, at, 1, 1 - i)

    parts = (
        [(near, i, 0, i // 2, i % 2) for i in range(8)],
        [(far, i, 1, (0, 1, 3)[i // 2], i % 2) for i in range(6)],
        [(last, i, 1, 2, i) for i in range(2)],
    )
    groups = (*parts, parts[0] + parts[1] + parts[2])
    first_line = vir[pl.ds((2 * col) % 8, 1), :]
    second_line = vir[pl.ds((2 * col + 1) % 8, 1), :]

    def chunk(group, k, dx):
        members = groups[group]
        unit = slot_k[k] if dx == 0 else CROSS + (dx - 1) * 4 + k
        there = line_k[k] * 4 + (x + dx) % 4
        uppers = [
            (1 - zh if half else zh) * 8 + ((y + dy) % 4) * 2 + (core + dc) % 2 for _, _, half, dy, dc in members
        ]
        lows = [sides[there, upper] for upper in uppers]
        dims = (((1,), (1,)), ((), ()))
        both = [
            lax.dot_general(
                jnp.concatenate([ref[i, piece, low] for (ref, i, *_), low in zip(members, lows)], axis=0),
                store[unit, 1 - piece].reshape(UNIT, DEPTH),
                dims,
                preferred_element_type=jnp.float32,
            )
            for piece in (0, 1)
        ]
        both = both[0] + both[1]
        level = occ_s[there * 4 + col // 4]
        for i, upper in enumerate(uppers):
            mine = both[i * BLOCK : (i + 1) * BLOCK]
            right = jnp.full((1, BLOCK), sides[GRID + there, GRID + upper])
            across = jnp.where(right > 0, second_line, first_line) - level
            kept = jnp.where(jnp.broadcast_to(right, (BLOCK, BLOCK)) > 0, mine[:, BLOCK:], mine[:, :BLOCK])
            below = gaps[upper * 2 + lows[i]] + across
            dense[there * GRID + upper] = (kept / below).astype(jnp.bfloat16)

    def compute(group, *todo):
        for first, step, count in todo:
            for at in range(first, first + step * count, step):
                chunk(group, at // 4, at % 4)

    def half_ready(h, dys):
        for dy in dys:
            for piece in (0, 1):
                got("c", h, dy, piece)

    for i in (0, 1):
        send("z", 0, 1, i)
        send("z", 1, 1, 1 - i)
        send("x", 0, 0, i)
        send("x", 0, 1, 1 - i)
        send("y", 0, 0, i)
        send("y", 0, 1, 1 - i)
    send("c", 0, 0, 0)
    send("c", 0, 0, 1)
    occ_copy.wait()
    for j in range(8):
        turned = jnp.broadcast_to(vir[j : j + 1, :], (BLOCK, BLOCK)).T
        for t in range(4):
            gaps[j + 8 * t] = turned - occ_s[row * 4 + t]
    dense[CELLS] = jnp.zeros((BLOCK, BLOCK), jnp.bfloat16)
    for flow in (0, 1):
        got("z", flow, 1, flow)
        send("z", flow, 2, flow)
        got("x", 0, flow, flow)
        send("xf", 0, flow)
        got("y", 0, flow, flow)
        send("yf", 0, flow)
    for flow in (0, 1):
        got("z", flow, 1, 1 - flow)
    send_unit("x", 1)
    for flow in (0, 1):
        got("y", 0, flow, 1 - flow)
    for dy in (1, 3):
        send("c", 0, dy, 0)
        send("c", 0, dy, 1)
    for flow in (0, 1):
        got("z", flow, 2, flow)
        send("z", flow, 3, flow)
    for flow in (0, 1):
        got("yf", 0, flow)
        send("c", 0, 2, flow)
    for flow in (0, 1):
        got("z", flow, 3, flow)
        send("z", flow, 4, flow)
        send("z", flow, 2, 1 - flow)
    for flow in (0, 1):
        got("x", 0, flow, 1 - flow)
        got("x", 1, flow, flow)
        send("xf", 1, flow)
    for flow in (0, 1):
        send("x", 2, flow, 0)
    for flow in (0, 1):
        got("z", flow, 4, flow)
    send_unit("y", 1)
    send("c", 1, 0, 0)
    send("c", 1, 0, 1)
    half_ready(0, range(4))
    compute(0, (0, 1, 2), (3, 1, 1))
    for flow in (0, 1):
        got("xf", 0, flow)
        got("x", 1, flow, 1 - flow)
    compute(0, (2, 2, 2))
    for flow in (0, 1):
        got("z", flow, 2, 1 - flow)
        send("z", flow, 3, 1 - flow)
    for flow in (0, 1):
        send("x", 2, flow, 1)
    send_line(1)
    for flow in (0, 1):
        got("y", 1, flow, flow)
        send("yf", 1, flow)
    compute(0, (5, 2, 2), (8, 1, 1))
    for flow in (0, 1):
        got("z", flow, 3, 1 - flow)
    send_unit("x", 3)
    for flow in (0, 1):
        got("y", 1, flow, 1 - flow)
    for dy in (1, 3):
        send("c", 1, dy, 0)
        send("c", 1, dy, 1)
    for flow in (0, 1):
        got("x", 2, flow, 0)
        got("x", 2, flow, 1)
    for flow in (0, 1):
        send("xf", 2, flow)
    compute(0, (12, 1, 1))
    half_ready(1, (0, 1, 3))
    compute(1, (0, 1, 2))
    got_line(1)
    send_line(2)
    for flow in (0, 1):
        got("yf", 1, flow)
        send("c", 1, 2, flow)
    compute(0, (9, 2, 2))
    compute(1, (2, 1, 4))
    for flow in (0, 1):
        got("x", 3, flow, flow)
        send("xf", 3, flow)
    compute(1, (7, 1, 2))
    got_line(2)
    send_line(3)
    for flow in (0, 1):
        got("xf", 1, flow)
    compute(0, (6, 1, 1))
    compute(1, (6, 1, 1), (9, 2, 2), (12, 1, 1))
    half_ready(1, (2,))
    compute(2, (0, 1, 10), (11, 1, 2))
    for flow in (0, 1):
        got("xf", 2, flow)
    compute(3, (10, 1, 1))
    for flow in (0, 1):
        got("x", 3, flow, 1 - flow)
    compute(3, (13, 2, 2))
    for flow in (0, 1):
        got("xf", 3, flow)
    got_line(3)
    compute(3, (14, 1, 1))

    for copy in started:
        copy.wait_send()
    for flow, dist in on_line:

        @pl.when(passes_on(flow, dist))
        def _(flow=flow, dist=dist):
            for piece in (0, 1):
                descriptor(("w", flow, dist, piece)).wait_send()


def products(sides, amplitudes, integrals, occ_energy, vir_energy):
    anywhere = pl.BlockSpec(memory_space=pl.ANY)
    vmem = pl.BlockSpec(memory_space=pltpu.VMEM)
    pairs = len(KEYS)
    return pl.pallas_call(
        exchange,
        out_shape=pltpu.VMEM((CELLS + 8, BLOCK, BLOCK), jnp.bfloat16),
        in_specs=[pl.BlockSpec(memory_space=pltpu.SMEM)] + [anywhere] * 4,
        out_specs=vmem,
        scratch_shapes=[
            pltpu.VMEM((UNITS, 2, 2, BLOCK, DEPTH), jnp.bfloat16),
            pltpu.VMEM((8, 2, 2, BLOCK, DEPTH), jnp.bfloat16),
            pltpu.VMEM((6, 2, 2, BLOCK, DEPTH), jnp.bfloat16),
            pltpu.VMEM((2, 2, 2, BLOCK, DEPTH), jnp.bfloat16),
            pltpu.VMEM((32, BLOCK, BLOCK), jnp.float32),
            pltpu.VMEM(vir_energy.shape, jnp.float32),
            pltpu.SMEM(occ_energy.shape, jnp.float32),
            pltpu.SemaphoreType.DMA((8,)),
            pltpu.SemaphoreType.DMA((pairs,)),
            pltpu.SemaphoreType.DMA((pairs,)),
        ],
        compiler_params=pltpu.CompilerParams(
            collective_id=0, has_side_effects=True, vmem_limit_bytes=LIMIT
        ),
        name="exchange",
    )(sides, amplitudes, integrals, occ_energy, vir_energy)


def ordered(ranks, dense, out, sem):
    def put(src, slot):
        pltpu.make_async_copy(dense.at[src], out.at[0, 0, slot], sem.at[0]).start()

    def some(t, count):
        for i in range(GRID):
            rank = ranks[t, i]

            @pl.when(rank > 0)
            def _():
                put(t * GRID + i, rank - 1)

            count = count + jnp.minimum(rank, 1)
        return count

    count = lax.fori_loop(0, GRID, some, jnp.int32(0))

    def rest(slot, carry):
        put(CELLS, slot)
        return carry

    lax.fori_loop(count, TILES, rest, 0)
    whole = dense.at[pl.ds(0, TILES)]
    pltpu.make_async_copy(whole, out.at[0, 0], sem.at[0]).wait()


def in_order(ranks, dense):
    anywhere = pl.BlockSpec(memory_space=pl.ANY)
    return pl.pallas_call(
        ordered,
        out_shape=jax.ShapeDtypeStruct((1, 1, TILES, BLOCK, BLOCK), jnp.bfloat16),
        in_specs=[pl.BlockSpec(memory_space=pltpu.SMEM), anywhere],
        out_specs=anywhere,
        scratch_shapes=[pltpu.SemaphoreType.DMA((1,))],
        compiler_params=pltpu.CompilerParams(vmem_limit_bytes=1024 * 1024),
        name="ordered",
    )(ranks, dense)


def shards(amplitudes, integrals, block_mask, occ_energy, vir_energy):
    col = lax.axis_index("col")

    def chosen(shape, test):
        down, across = (lax.broadcasted_iota(jnp.int32, shape, axis) for axis in (0, 1))
        return test(down, across).astype(jnp.float32)

    pick = chosen((32, 512), lambda v, at: at == v // 2 * 32 + 2 * col + v % 2)
    cell = lax.dot_general(pick, block_mask.astype(jnp.float32), (((1,), (1,)), ((), ())))
    rows = chosen((GRID, 32), lambda r, v: v // 2 == r)
    lines = chosen((32, GRID), lambda u, c: u // 2 == c)
    all_rows = chosen((32, 32), lambda r, v: jnp.where(r < GRID, v // 2 == r, v == 2 * (r - GRID) + 1))
    all_lines = chosen((32, 32), lambda u, c: jnp.where(c < GRID, u == 2 * c + 1, u // 2 == c - GRID))
    sides = (all_rows @ (cell @ all_lines)).astype(jnp.int32)
    upto = chosen((32, 32), lambda v, at: at <= v) @ cell
    upto = upto + jnp.sum(cell, axis=0, keepdims=True) @ chosen((32, 32), lambda at, u: at < u)
    ranks = (rows @ ((cell * upto) @ lines)).astype(jnp.int32)
    dense = products(
        sides,
        amplitudes.reshape(2, BLOCK, DEPTH),
        integrals.reshape(2, BLOCK, DEPTH),
        occ_energy,
        vir_energy.reshape(8, BLOCK),
    )
    return in_order(ranks, dense)


def solution(mesh):
    in_specs = (P(("row", "col"), None), P(("row", "col"), None), P("row", None), P(), P())
    out_specs = P("row", "col", None, None, None)
    return jax.shard_map(shards, mesh=mesh, in_specs=in_specs, out_specs=out_specs, check_vma=False)
```
